32 devices in a mesh: grp: 2 (over y), smp: 4 (over z), mrk: 4 (over x, core).
Axes of the slice: x: 2, y: 2, z: 4, core: 2. Of those that a mesh axis runs over, the one named last changes fastest.
Arguments:
- genotypes: bfloat16 [4096, 16384], P('smp', ('grp', 'mrk')), parts along dimension 1, may hold values from 0 to 2, as said below
- effect_class: int32 [16384], P(('grp', 'mrk')), parts along dimension 0, may hold values from 0 to 511
- effect_table: bfloat16 [1024, 256], P('grp'), parts along dimension 0, may hold values from -0.0625 to 0.0625
Outputs:
- assoc: float32 [256, 16384], P('smp', ('grp', 'mrk')), parts along dimension 1
The draws below stay inside these ranges and needn't reach their ends.
There are 2 independent parts, one for each index of `grp`. The reference program is written for one: setup_inputs(seed, part) draws one part's arguments, and reference() takes and returns one part's arrays. A program takes and returns all parts, laid end to end along the dimension named above; each array names one. Nothing has to cross between parts.
Inputs may be any that keep to these rules, and one draw needn't show every extreme that they name: `genotypes`: dosages are whole numbers.
All inputs are finite; a program needn't handle non-finite values.
Results may differ from the reference program's by a relative error of at most 0.0032.
Values may be sent and summed in bfloat16 or wider, within the bound.
No kernel may reach another device: no remote copies, remote signals or barrier semaphores. Data moves between devices by JAX's collectives and lax.ppermute only.
A program may use at most 64 MiB of HBM per device.

```python
import math
import jax
import jax.numpy as jnp
from jax import lax

PHENO = 256
CLASSES = 512
SAMPLES = 4096
MARKERS = 8192


def draw_genotypes(key, part):
    freq_key, sign_key, bits_key = jax.random.split(key, 3)
    frequency = jax.random.randint(freq_key, (1, MARKERS), 100, 360)
    direction = jax.random.randint(sign_key, (1, MARKERS), 0, 2)
    sample_rows = jnp.arange(SAMPLES, dtype=jnp.int32)[:, None]
    ancestry = 512 + 1024 * sample_rows // SAMPLES
    ancestry = jnp.where(direction == 1, ancestry, 2047 - ancestry)
    limits = frequency * ancestry // 32
    random_bits = jax.random.randint(bits_key, (SAMPLES, MARKERS), 0, 1 << 30)
    allele_one = (random_bits % 32768 < limits).astype(jnp.int32)
    allele_two = (random_bits // 32768 < limits).astype(jnp.int32)
    return (allele_one + allele_two).astype(jnp.bfloat16)


def with_ends(array, own_key, least, high):
    index_at = [jax.random.randint(jax.random.fold_in(own_key, axis), (), 0, length) for axis, length in enumerate(array.shape)]
    widest = array.shape.index(max(array.shape))
    beside = index_at[:widest] + [(index_at[widest] + 1) % array.shape[widest]] + index_at[widest + 1:]
    return array.at[tuple(index_at)].set(least).at[tuple(beside)].set(high)


def normal_values(stream_key, dims, width, limit, held_as=jnp.bfloat16):
    return jnp.clip(width * jax.random.normal(stream_key, dims, jnp.float32), -limit, limit).astype(held_as)


def setup_inputs(seed: int = 0, part: int = 0) -> dict:
    arg_keys = jax.random.split(jax.random.key(seed), 4)
    part_splits = jax.random.split(jax.random.fold_in(arg_keys[3], part), 4)
    genotypes = draw_genotypes(jax.random.fold_in(jax.random.fold_in(arg_keys[3], part), 71), part)
    effect_class = with_ends(jax.random.randint(part_splits[1], (MARKERS,), 0, CLASSES), jax.random.fold_in(part_splits[1], 1), 0, CLASSES - 1).astype(jnp.int32)
    effect_table = normal_values(part_splits[2], (CLASSES, PHENO), MARKERS ** -0.5, 0.0625)
    return dict(genotypes=genotypes, effect_class=effect_class, effect_table=effect_table)


EPSILON = 1e-05

def reference(genotypes, effect_class, effect_table):
    samples = genotypes.shape[0]
    totals = lax.optimization_barrier(jnp.sum(genotypes, axis=0, dtype=jnp.float32))
    allele_mean = totals / samples
    centered = lax.optimization_barrier(jnp.sum(jnp.square(genotypes.astype(jnp.float32) - allele_mean[None, :]), axis=0))
    inverse_spread = lax.rsqrt(centered / samples + EPSILON)
    effects = jnp.take(effect_table, effect_class, axis=0)
    scaled = (effects.astype(jnp.float32) * inverse_spread[:, None]).astype(jnp.bfloat16)
    phenotype = jnp.dot(genotypes, scaled, preferred_element_type=jnp.float32)
    center = lax.optimization_barrier(jnp.sum(phenotype, axis=0)) / samples
    spread = lax.optimization_barrier(jnp.sum(jnp.square(phenotype - center[None, :]), axis=0)) / samples
    standard = ((phenotype - center[None, :]) * lax.rsqrt(spread + EPSILON)[None, :]).astype(jnp.bfloat16)
    summed = jnp.dot(standard.T, genotypes, preferred_element_type=jnp.float32)
    root_count = math.sqrt(samples)
    return summed * inverse_spread[None, :] / root_count
```

```python
import functools
import math

import jax
import jax.numpy as jnp
from jax import lax
from jax.experimental import pallas as pl
from jax.experimental.pallas import tpu as pltpu
from jax.sharding import PartitionSpec as P

EPSILON = 1e-05
LANES = 128
F32 = jnp.float32
BF16 = jnp.bfloat16


def vmem(count):
    return [pl.BlockSpec(memory_space=pltpu.VMEM)] * count


def call(body, out_shape, inputs, flops=0, moved=0, scratch=(), scalars=0, spaces=None):
    specs = [pl.BlockSpec(memory_space=pltpu.SMEM)] * scalars
    specs += spaces if spaces else vmem(len(inputs) - scalars)
    many = isinstance(out_shape, (list, tuple))
    return pl.pallas_call(
        body,
        out_shape=out_shape,
        in_specs=specs,
        out_specs=vmem(len(out_shape)) if many else pl.BlockSpec(memory_space=pltpu.VMEM),
        scratch_shapes=list(scratch),
        cost_estimate=pl.CostEstimate(flops=flops, bytes_accessed=moved, transcendentals=0),
        compiler_params=pltpu.CompilerParams(vmem_limit_bytes=40 << 20),
    )(*inputs)


def stats_body(g_hbm, o_ref, g_ref, sems, *, chunks):
    rows, cols = g_ref.shape
    step = rows // chunks
    copies = [
        pltpu.make_async_copy(
            g_hbm.at[pl.ds(k * step, step), :], g_ref.at[pl.ds(k * step, step), :], sems.at[k]
        )
        for k in range(chunks)
    ]
    for copy in copies:
        copy.start()
    one = jnp.zeros((16, cols), BF16)
    two = jnp.zeros((16, cols), BF16)
    total = jnp.zeros((1, cols), F32)
    square = jnp.zeros((1, cols), F32)
    for k in range(chunks):
        copies[k].wait()
        for r in range(k * step, (k + 1) * step, 16):
            tile = g_ref[r : r + 16, :]
            one = one + tile
            two = two + tile * tile
            if (r // 16 + 1) % 64 == 0 or r + 16 == rows:
                total = total + jnp.sum(one.astype(F32), axis=0, keepdims=True)
                square = square + jnp.sum(two.astype(F32), axis=0, keepdims=True)
                one = jnp.zeros((16, cols), BF16)
                two = jnp.zeros((16, cols), BF16)
    o_ref[0:1, :] = total
    o_ref[1:2, :] = square


def effects_body(class_ref, table_ref, o_ref):
    classes = table_ref.shape[0]
    markers = class_ref.shape[1]
    width = 512
    for start in range(0, markers, width):
        stop = min(markers, start + width)
        ids = lax.broadcasted_iota(jnp.int32, (classes, stop - start), 0)
        onehot = (ids == class_ref[0:1, start:stop]).astype(F32).astype(BF16)
        o_ref[:, start:stop] = lax.dot_general(
            table_ref[...], onehot, (((0,), (0,)), ((), ())), preferred_element_type=F32
        ).astype(BF16)


def moments(stats, samples):
    total = stats[0:1, :]
    square = stats[1:2, :]
    wide = samples * square.astype(jnp.int32) - total.astype(jnp.int32) * total.astype(jnp.int32)
    variance = wide.astype(F32) / (samples * samples)
    return total / samples, lax.rsqrt(variance + EPSILON)


def phenotype_body(core_ref, *refs, samples, peers):
    stat_refs, (effect_ref, g_ref, send_ref, keep_ref, moment_ref) = refs[:peers], refs[peers:]
    stats = stat_refs[0][...]
    for ref in stat_refs[1:]:
        stats = stats + ref[...]
    mean, inverse_spread = moments(stats, samples)
    moment_ref[0:1, :] = mean
    moment_ref[1:2, :] = inverse_spread
    half = effect_ref.shape[0] // 2
    width = min(256, g_ref.shape[0])
    core = core_ref[0]
    for part, out_ref in ((1 - core, send_ref), (core, keep_ref)):
        rows = effect_ref[pl.ds(pl.multiple_of(part * half, half), half), :]
        scaled = (rows.astype(F32) * inverse_spread).astype(BF16)
        center = jnp.sum(scaled.astype(F32) * mean, axis=1, keepdims=True)
        for start in range(0, g_ref.shape[0], width):
            block = lax.dot_general(
                scaled, g_ref[start : start + width, :], (((1,), (1,)), ((), ())),
                preferred_element_type=F32,
            )
            out_ref[:, start : start + width] = (block - center).astype(out_ref.dtype)


def product_body(where_ref, *refs, wire):
    c_ref, moment_ref, g_ref, out_ref = refs
    rows = out_ref.shape[0]
    cols = g_ref.shape[1]
    start = pl.multiple_of(where_ref[0] * rows, rows)
    c = c_ref[pl.ds(start, rows), :]
    wide = c.astype(F32)
    total = jnp.sum(wide, axis=1, keepdims=True)
    square = jnp.sum(wide * wide, axis=1, keepdims=True)
    width = min(512, cols)
    for at in range(0, cols, width):
        block = jnp.dot(c, g_ref[:, at : at + width], preferred_element_type=F32)
        block = block - total * moment_ref[0:1, at : at + width]
        out_ref[:, at : at + width] = block.astype(out_ref.dtype)
    lane = lax.broadcasted_iota(jnp.int32, (rows, LANES), 1)
    high = square.astype(BF16).astype(F32)
    if wire:
        out_ref[:, cols:] = jnp.where(lane == 0, high, square - high).astype(out_ref.dtype)
    else:
        out_ref[:, cols:] = jnp.where(lane == 0, square, jnp.zeros_like(square))


def finish_body(*refs, samples):
    moment_ref, out_ref = refs[-2:]
    pieces = refs[:-2]
    cols = out_ref.shape[1]
    tail = pieces[0][:, cols:].astype(F32)
    for piece in pieces[1:]:
        tail = tail + piece[:, cols:].astype(F32)
    spread = (tail[:, 0:1] + tail[:, 1:2]) / samples
    scale = lax.rsqrt(spread + EPSILON) / math.sqrt(samples)
    width = min(512, cols)
    for at in range(0, cols, width):
        total = pieces[0][:, at : at + width].astype(F32)
        for piece in pieces[1:]:
            total = total + piece[:, at : at + width].astype(F32)
        out_ref[:, at : at + width] = total * scale * moment_ref[1:2, at : at + width]


def shape(dims, dtype):
    return jax.ShapeDtypeStruct(dims, dtype)


def xor_pairs(size, k):
    return [(i, i ^ k) for i in range(size)]


def exchange(x, axis, k):
    return lax.ppermute(x, axis, xor_pairs(lax.axis_size(axis), k))


def marker_stats(genotypes):
    rows, cols = genotypes.shape
    chunks = 8
    return call(
        functools.partial(stats_body, chunks=chunks),
        shape((2, cols), F32),
        [genotypes],
        moved=2 * rows * cols,
        scratch=[pltpu.VMEM((rows, cols), BF16), pltpu.SemaphoreType.DMA((chunks,))],
        spaces=[pl.BlockSpec(memory_space=pl.ANY)],
    )


def small_mesh(genotypes, effect_class, effect_table):
    peers = lax.axis_size("smp")
    samples = genotypes.shape[0] * peers
    here, markers = genotypes.shape
    pheno = effect_table.shape[1]
    half, share = pheno // 2, pheno // peers
    me = lax.axis_index("smp")
    core = (lax.axis_index("mrk") % 2).reshape(1)

    stats = marker_stats(genotypes)
    others = [exchange(stats, "smp", k) for k in range(1, peers)]
    effects = call(
        effects_body, shape((pheno, markers), BF16),
        [effect_class.reshape(1, markers), effect_table],
        flops=2 * pheno * markers * effect_table.shape[0], moved=4 * pheno * markers,
    )
    send, keep, moment = call(
        functools.partial(phenotype_body, samples=samples, peers=peers),
        [shape((half, here), BF16), shape((half, here), F32), shape((2, markers), F32)],
        [core, stats, *others, effects, genotypes],
        flops=2 * pheno * here * markers, moved=2 * here * markers, scalars=1,
    )
    keep = keep + exchange(send, "mrk", 1).astype(F32)
    keep = (keep + exchange(keep.astype(BF16), "mrk", 2).astype(F32)).astype(BF16)
    other = exchange(keep, "mrk", 1)
    first = jnp.where(core[0] == 0, keep, other)
    second = jnp.where(core[0] == 0, other, keep)
    c = jnp.concatenate([first, second], axis=0)

    def product(where, wire):
        return call(
            functools.partial(product_body, wire=wire),
            shape((share, markers + LANES), BF16 if wire else F32),
            [where.reshape(1), c, moment, genotypes],
            flops=2 * share * here * markers, moved=2 * here * markers, scalars=1,
        )

    arrived = [exchange(product(me ^ k, True), "smp", k) for k in (3, 2, 1)]
    mine = product(me, False)
    return call(
        functools.partial(finish_body, samples=samples),
        shape((share, markers), F32),
        [mine, *arrived, moment], moved=8 * share * markers,
    )


def any_mesh(genotypes, effect_class, effect_table):
    samples = genotypes.shape[0] * lax.axis_size("smp")
    here, markers = genotypes.shape
    mean, inverse_spread = moments(lax.psum(marker_stats(genotypes), "smp"), samples)
    effects = call(
        effects_body, shape((effect_table.shape[1], markers), BF16),
        [effect_class.reshape(1, markers), effect_table],
    )
    scaled = (effects.astype(F32) * inverse_spread).astype(BF16)
    center = jnp.sum(scaled.astype(F32) * mean, axis=1, keepdims=True)
    partial_sum = lax.dot_general(
        scaled, genotypes, (((1,), (1,)), ((), ())), preferred_element_type=F32
    )
    c = lax.psum(partial_sum - center, "mrk")
    spread = lax.psum(jnp.sum(jnp.square(c), axis=1, keepdims=True), "smp") / samples
    standard = (c * lax.rsqrt(spread + EPSILON)).astype(BF16)
    summed = lax.psum_scatter(
        jnp.dot(standard, genotypes, preferred_element_type=F32),
        "smp", scatter_dimension=0, tiled=True,
    )
    return summed * inverse_spread / math.sqrt(samples)


def solution(mesh):
    small = mesh.shape["smp"] == 4 and mesh.shape["mrk"] == 4
    return jax.shard_map(
        small_mesh if small else any_mesh,
        mesh=mesh,
        in_specs=(P("smp", ("grp", "mrk")), P(("grp", "mrk")), P("grp", None)),
        out_specs=P("smp", ("grp", "mrk")),
        check_vma=False,
    )
```

```python
import functools
import math

import jax
import jax.numpy as jnp
from jax import lax
from jax.experimental import pallas as pl
from jax.experimental.pallas import tpu as pltpu
from jax.sharding import PartitionSpec as P

EPSILON = 1e-05
LANES = 128
F32 = jnp.float32
BF16 = jnp.bfloat16
HBM = pltpu.MemorySpace.HBM


def vmem(count):
    return [pl.BlockSpec(memory_space=pltpu.VMEM)] * count


def call(body, out_shape, inputs, flops=0, moved=0, scratch=(), spaces=None, limit=4):
    many = isinstance(out_shape, (list, tuple))
    return pl.pallas_call(
        body,
        out_shape=out_shape,
        in_specs=spaces or vmem(len(inputs)),
        out_specs=vmem(len(out_shape)) if many else pl.BlockSpec(memory_space=pltpu.VMEM),
        scratch_shapes=list(scratch),
        cost_estimate=pl.CostEstimate(flops=flops, bytes_accessed=moved, transcendentals=0),
        compiler_params=pltpu.CompilerParams(vmem_limit_bytes=limit << 20),
    )(*inputs)


def shape(dims, dtype):
    return jax.ShapeDtypeStruct(dims, dtype)


def add_moments(tile_rows, g_ref, start, stop, total, square):
    cols = g_ref.shape[1]
    for base in range(start, stop, 16 * tile_rows):
        one = jnp.zeros((16, cols), BF16)
        two = jnp.zeros((16, cols), BF16)
        for row in range(base, min(stop, base + 16 * tile_rows), 16):
            tile = g_ref[row : row + 16, :]
            one = one + tile
            two = two + tile * tile
        total = total + jnp.sum(one.astype(F32), axis=0, keepdims=True)
        square = square + jnp.sum(two.astype(F32), axis=0, keepdims=True)
    return total, square


def stats_body(g_hbm, o_ref, g_ref, sems):
    rows, cols = g_ref.shape
    chunks = sems.shape[0]
    step = rows // chunks
    copies = [
        pltpu.make_async_copy(
            g_hbm.at[pl.ds(k * step, step), :], g_ref.at[pl.ds(k * step, step), :], sems.at[k]
        )
        for k in range(chunks)
    ]
    for copy in copies:
        copy.start()
    total = jnp.zeros((1, cols), F32)
    square = jnp.zeros((1, cols), F32)
    for k in range(chunks):
        copies[k].wait()
        total, square = add_moments(64, g_ref, k * step, (k + 1) * step, total, square)
    o_ref[0:1, :] = total
    o_ref[1:2, :] = square


def marker_stats(genotypes):
    rows, cols = genotypes.shape
    return call(
        stats_body,
        [shape((2, cols), F32), shape((rows, cols), BF16)],
        [genotypes],
        moved=2 * rows * cols,
        scratch=[pltpu.SemaphoreType.DMA((8,))],
        spaces=[pl.BlockSpec(memory_space=HBM)],
        limit=12,
    )


def effects_body(class_ref, table_ref, o_ref):
    classes = table_ref.shape[0]
    markers = class_ref.shape[1]
    width = 512
    for start in range(0, markers, width):
        stop = min(markers, start + width)
        ids = lax.broadcasted_iota(jnp.int32, (classes, stop - start), 0)
        onehot = (ids == class_ref[0:1, start:stop]).astype(F32).astype(BF16)
        o_ref[:, start:stop] = lax.dot_general(
            table_ref[...], onehot, (((0,), (0,)), ((), ())), preferred_element_type=F32
        ).astype(BF16)


def marker_effects(effect_class, effect_table):
    classes, pheno = effect_table.shape
    markers = effect_class.shape[0]
    return call(
        effects_body, shape((pheno, markers), BF16),
        [effect_class.reshape(1, markers), effect_table],
        flops=2 * pheno * markers * classes, moved=4 * pheno * markers,
    )


def moments(stats, samples):
    total = stats[0:1, :]
    square = stats[1:2, :]
    wide = samples * square.astype(jnp.int32) - total.astype(jnp.int32) * total.astype(jnp.int32)
    variance = wide.astype(F32) / (samples * samples)
    return total / samples, lax.rsqrt(variance + EPSILON)


FIRST = ((3, 2), (0, 3), (3, 0), (0, 1))
SECOND = ((1, 0), (2, 1), (1, 2), (2, 3))


def place():
    return lax.axis_index("smp"), lax.axis_index("mrk") % 2


def block_of(table, z, core):
    found = jnp.int32(0)
    for i, row in enumerate(table):
        for j, value in enumerate(row):
            found = jnp.where((z == i) & (core == j), jnp.int32(value), found)
    return found


def partial_body(*refs, plan, samples, peers):
    stat_refs, effect_ref, g_ref, out_refs = (
        refs[:peers], refs[peers], refs[peers + 1], refs[peers + 2 :],
    )
    stats = stat_refs[0][...]
    for ref in stat_refs[1:]:
        stats = stats + ref[...]
    mean, inverse_spread = moments(stats, samples)
    if len(out_refs) > len(plan):
        out_refs[-1][0:1, :] = mean
        out_refs[-1][1:2, :] = inverse_spread
    z, core = place()
    share = out_refs[0].shape[0]
    scaled, centers = [], []
    for table, mine in plan:
        block = block_of(table, z, core if mine else 1 - core)
        rows = effect_ref[pl.ds(pl.multiple_of(block * share, share), share), :]
        one = (rows.astype(F32) * inverse_spread).astype(BF16)
        scaled.append(one)
        centers.append(jnp.sum(one.astype(F32) * mean, axis=1, keepdims=True))
    left = jnp.concatenate(scaled, axis=0) if len(plan) > 1 else scaled[0]
    width = min(256, g_ref.shape[0])
    for at in range(0, g_ref.shape[0], width):
        product = lax.dot_general(
            left, g_ref[at : at + width, :], (((1,), (1,)), ((), ())), preferred_element_type=F32
        )
        for k, center in enumerate(centers):
            piece = product[k * share : (k + 1) * share] - center
            out_refs[k][:, at : at + width] = piece.astype(out_refs[k].dtype)


def chip_sum_body(keep_ref, arrived_ref, sum_ref, wire_ref):
    total = keep_ref[...] + arrived_ref[...].astype(F32)
    sum_ref[...] = total
    wire_ref[...] = total.astype(BF16)


def full_sum_body(keep_ref, arrived_ref, c_ref):
    c_ref[...] = (keep_ref[...] + arrived_ref[...].astype(F32)).astype(BF16)


def product(c, moment_ref, g_ref, out_refs, extra_ref=None):
    rows, cols = c.shape[0], g_ref.shape[1]
    wide = c.astype(F32)
    total = jnp.sum(wide, axis=1, keepdims=True)
    square = jnp.sum(wide * wide, axis=1, keepdims=True)
    width = min(512, cols)
    for at in range(0, cols, width):
        block = jnp.dot(c, g_ref[:, at : at + width], preferred_element_type=F32)
        block = block - total * moment_ref[0:1, at : at + width]
        if extra_ref is not None:
            block = block + extra_ref[:, at : at + width].astype(F32)
        for out_ref in out_refs:
            out_ref[:, at : at + width] = block.astype(out_ref.dtype)
    if extra_ref is not None:
        square = square + tail_sum(extra_ref)
    for out_ref in out_refs:
        put_tail(out_ref, square)


def tail_sum(ref):
    tail = ref[:, ref.shape[1] - LANES :].astype(F32)
    return tail[:, 0:1] + tail[:, 1:2]


def put_tail(ref, square):
    high = square.astype(BF16).astype(F32)
    lane = lax.broadcasted_iota(jnp.int32, (ref.shape[0], LANES), 1)
    tail = jnp.where(lane == 0, high, square - high)
    ref[:, ref.shape[1] - LANES :] = tail.astype(ref.dtype)


def product_body(c_ref, moment_ref, g_ref, *out_refs):
    product(c_ref[...], moment_ref, g_ref, out_refs)


def pick(a_ref, b_ref, first):
    return jnp.where(first, a_ref[...].astype(F32), b_ref[...].astype(F32)).astype(BF16)


def third_body(own_ref, other_ref, held_ref, one_ref, moment_ref, g_ref, out_ref):
    z, core = place()
    edge = (z == 0) | (z == 3)

    @pl.when(edge)
    def _():
        product(pick(own_ref, other_ref, core == 0), moment_ref, g_ref, [out_ref])

    @pl.when(jnp.logical_not(edge) & (core == 0))
    def _():
        out_ref[...] = (held_ref[...] + one_ref[...].astype(F32)).astype(BF16)
        put_tail(out_ref, tail_sum(held_ref) + tail_sum(one_ref))

    @pl.when(jnp.logical_not(edge) & (core == 1))
    def _():
        out_ref[...] = held_ref[...].astype(BF16)


def fourth_body(own_ref, other_ref, one_ref, two_ref, moment_ref, g_ref, out_ref):
    z, core = place()
    middle = (z == 1) | (z == 2)

    @pl.when(middle & (core == 0))
    def _():
        product(own_ref[...], moment_ref, g_ref, [out_ref], two_ref)

    @pl.when(middle & (core == 1))
    def _():
        product(other_ref[...], moment_ref, g_ref, [out_ref], one_ref)

    @pl.when(jnp.logical_not(middle))
    def _():
        out_ref[...] = jnp.zeros_like(out_ref)


def last_body(own_ref, other_ref, moment_ref, g_ref, out_ref):
    _, core = place()
    product(pick(own_ref, other_ref, core == 1), moment_ref, g_ref, [out_ref])


def finish_body(mine_ref, one_ref, two_ref, three_ref, four_ref, moment_ref, out_ref, *, samples):
    z, _ = place()
    cols = out_ref.shape[1]
    edge = (z == 0) | (z == 3)

    def finish(refs):
        square = tail_sum(refs[0])
        for ref in refs[1:]:
            square = square + tail_sum(ref)
        scale = lax.rsqrt(square / samples + EPSILON) / math.sqrt(samples)
        width = min(512, cols)
        for at in range(0, cols, width):
            total = refs[0][:, at : at + width].astype(F32)
            for ref in refs[1:]:
                total = total + ref[:, at : at + width].astype(F32)
            out_ref[:, at : at + width] = total * scale * moment_ref[1:2, at : at + width]

    @pl.when(edge)
    def _():
        finish([mine_ref, one_ref, two_ref, three_ref])

    @pl.when(jnp.logical_not(edge))
    def _():
        finish([mine_ref, three_ref, four_ref])


def exchange(x, axis, k):
    return lax.ppermute(x, axis, [(i, i ^ k) for i in range(lax.axis_size(axis))])


def routed(x, *routes):
    peers = lax.axis_size("mrk")
    pairs = [
        (source * peers + m, target * peers + m)
        for m in range(peers)
        for source, target in routes[m % 2]
    ]
    return lax.ppermute(x, ("smp", "mrk"), pairs)


def small_mesh(genotypes, effect_class, effect_table):
    peers = lax.axis_size("smp")
    samples = genotypes.shape[0] * peers
    here, markers = genotypes.shape
    pheno = effect_table.shape[1]
    share = pheno // peers
    work = 2 * share * here * markers

    stats, held = marker_stats(genotypes)
    stats = [stats] + [exchange(stats, "smp", k) for k in (3, 2, 1)]
    effects = marker_effects(effect_class, effect_table)

    def partials(plan, types, with_moment=False):
        outs = [shape((share, here), t) for t in types]
        if with_moment:
            outs.append(shape((2, markers), F32))
        return call(
            functools.partial(partial_body, plan=plan, samples=samples, peers=peers),
            outs, [*stats, effects, held], flops=len(plan) * work, moved=2 * here * markers,
        )

    def chip_sum(keep, arrived):
        return call(chip_sum_body, [shape((share, here), F32), shape((share, here), BF16)], [keep, arrived])

    def full_sum(keep, arrived):
        return call(full_sum_body, shape((share, here), BF16), [keep, arrived])

    send_a, moment = partials([(FIRST, False)], [BF16], True)
    cross_a = exchange(send_a, "mrk", 1)
    keep_a, send_b = partials([(FIRST, True), (SECOND, False)], [F32, BF16])
    sum_a, wire_a = chip_sum(keep_a, cross_a)
    far_a = exchange(wire_a, "mrk", 2)
    cross_b = exchange(send_b, "mrk", 1)
    (keep_b,) = partials([(SECOND, True)], [F32])
    sum_b, wire_b = chip_sum(keep_b, cross_b)
    far_b = exchange(wire_b, "mrk", 2)

    piece = shape((share, markers + LANES), BF16)
    piece_wide = shape((share, markers + LANES), F32)

    def make(body, outs, inputs):
        return call(body, outs, [*inputs, moment, held], flops=work, moved=2 * here * markers)

    own_a = full_sum(sum_a, far_a)
    (go1,) = make(product_body, [piece], [own_a])
    got1 = routed(go1, ((0, 1), (1, 0), (2, 3), (3, 2)), ((0, 1), (1, 3), (2, 0), (3, 2)))
    other_a = exchange(own_a, "mrk", 1)
    go2, wait3 = make(product_body, [piece, piece_wide], [other_a])
    got2 = routed(go2, ((0, 1), (3, 2)), ((0, 3), (3, 0)))
    own_b = full_sum(sum_b, far_b)
    other_b = exchange(own_b, "mrk", 1)
    go3 = make(third_body, piece, [own_b, other_b, wait3, got1])
    got3 = routed(go3, ((0, 1), (1, 3), (2, 0), (3, 2)), ((0, 1), (1, 0), (2, 3), (3, 2)))
    go4 = make(fourth_body, piece, [own_b, other_b, got1, got2])
    got4 = routed(go4, ((1, 2), (2, 1)), ((1, 2), (2, 1)))
    mine = make(last_body, piece_wide, [own_b, other_b])
    return call(
        functools.partial(finish_body, samples=samples),
        shape((share, markers), F32),
        [mine, got1, got2, got3, got4, moment], moved=8 * share * markers,
    )


def any_mesh(genotypes, effect_class, effect_table):
    samples = genotypes.shape[0] * lax.axis_size("smp")
    mean, inverse_spread = moments(lax.psum(marker_stats(genotypes)[0], "smp"), samples)
    effects = marker_effects(effect_class, effect_table)
    scaled = (effects.astype(F32) * inverse_spread).astype(BF16)
    center = jnp.sum(scaled.astype(F32) * mean, axis=1, keepdims=True)
    partial_sum = lax.dot_general(
        scaled, genotypes, (((1,), (1,)), ((), ())), preferred_element_type=F32
    )
    c = lax.psum(partial_sum - center, "mrk")
    spread = lax.psum(jnp.sum(jnp.square(c), axis=1, keepdims=True), "smp") / samples
    standard = (c * lax.rsqrt(spread + EPSILON)).astype(BF16)
    summed = lax.psum_scatter(
        jnp.dot(standard, genotypes, preferred_element_type=F32),
        "smp", scatter_dimension=0, tiled=True,
    )
    return summed * inverse_spread / math.sqrt(samples)


def solution(mesh):
    small = mesh.shape["smp"] == 4 and mesh.shape["mrk"] == 4
    return jax.shard_map(
        small_mesh if small else any_mesh,
        mesh=mesh,
        in_specs=(P("smp", ("grp", "mrk")), P(("grp", "mrk")), P("grp", None)),
        out_specs=P("smp", ("grp", "mrk")),
        check_vma=False,
    )
```

```python
import functools
import math

import jax
import jax.numpy as jnp
from jax import lax
from jax.experimental import pallas as pl
from jax.experimental.pallas import tpu as pltpu
from jax.sharding import PartitionSpec as P

EPSILON = 1e-05
LANES = 128
TAIL = 16
F32 = jnp.float32
BF16 = jnp.bfloat16
HBM = pltpu.MemorySpace.HBM
LOAD_LIMIT = 12


def vmem(count):
    return [pl.BlockSpec(memory_space=pltpu.VMEM)] * count


def call(body, out_shape, inputs, flops=0, moved=0, scratch=(), spaces=None, limit=4, out_spaces=None):
    many = isinstance(out_shape, (list, tuple))
    return pl.pallas_call(
        body,
        out_shape=out_shape,
        in_specs=spaces or vmem(len(inputs)),
        out_specs=out_spaces or (vmem(len(out_shape)) if many else vmem(1)[0]),
        scratch_shapes=list(scratch),
        cost_estimate=pl.CostEstimate(flops=flops, bytes_accessed=moved, transcendentals=0),
        compiler_params=pltpu.CompilerParams(vmem_limit_bytes=limit << 20),
    )(*inputs)


def shape(dims, dtype):
    return jax.ShapeDtypeStruct(dims, dtype)


def add_moments(tile_rows, g_ref, start, stop, total, square):
    cols = g_ref.shape[1]
    for base in range(start, stop, 16 * tile_rows):
        one = jnp.zeros((16, cols), BF16)
        two = jnp.zeros((16, cols), BF16)
        for row in range(base, min(stop, base + 16 * tile_rows), 16):
            tile = g_ref[row : row + 16, :]
            one = one + tile
            two = two + tile * tile
        total = total + jnp.sum(one.astype(F32), axis=0, keepdims=True)
        square = square + jnp.sum(two.astype(F32), axis=0, keepdims=True)
    return total, square


def stats_body(g_hbm, o_ref, g_ref, sems):
    rows, cols = g_ref.shape
    chunks = sems.shape[0]
    step = rows // chunks
    copies = [
        pltpu.make_async_copy(
            g_hbm.at[pl.ds(k * step, step), :], g_ref.at[pl.ds(k * step, step), :], sems.at[k]
        )
        for k in range(chunks)
    ]
    for copy in copies:
        copy.start()
    total = jnp.zeros((1, cols), F32)
    square = jnp.zeros((1, cols), F32)
    for k in range(chunks):
        copies[k].wait()
        total, square = add_moments(64, g_ref, k * step, (k + 1) * step, total, square)
    o_ref[0:1, :] = total
    o_ref[1:2, :] = square


def marker_stats(genotypes):
    rows, cols = genotypes.shape
    return call(
        stats_body,
        [shape((2, cols), F32), shape((rows, cols), BF16)],
        [pltpu.with_memory_space_constraint(genotypes, HBM)],
        moved=2 * rows * cols,
        scratch=[pltpu.SemaphoreType.DMA((8,))],
        spaces=[pl.BlockSpec(memory_space=HBM)],
        limit=LOAD_LIMIT,
    )


def effects_body(class_ref, table_ref, o_ref):
    classes = table_ref.shape[0]
    markers = class_ref.shape[1]
    width = 512
    for start in range(0, markers, width):
        stop = min(markers, start + width)
        ids = lax.broadcasted_iota(jnp.int32, (classes, stop - start), 0)
        onehot = (ids == class_ref[0:1, start:stop]).astype(F32).astype(BF16)
        o_ref[:, start:stop] = lax.dot_general(
            table_ref[...], onehot, (((0,), (0,)), ((), ())), preferred_element_type=F32
        ).astype(BF16)


def marker_effects(effect_class, effect_table):
    classes, pheno = effect_table.shape
    markers = effect_class.shape[0]
    return call(
        effects_body, shape((pheno, markers), BF16),
        [effect_class.reshape(1, markers), effect_table],
        flops=2 * pheno * markers * classes, moved=4 * pheno * markers,
    )


def moments(stats, samples):
    total = stats[0:1, :]
    square = stats[1:2, :]
    wide = samples * square.astype(jnp.int32) - total.astype(jnp.int32) * total.astype(jnp.int32)
    variance = wide.astype(F32) / (samples * samples)
    return total / samples, lax.rsqrt(variance + EPSILON)


FIRST = ((3, 2), (2, 3), (1, 0), (0, 1))
SECOND = ((1, 0), (0, 1), (3, 2), (2, 3))


def place():
    return lax.axis_index("smp"), lax.axis_index("mrk") % 2


def block_of(table, z, core):
    found = jnp.int32(0)
    for i, row in enumerate(table):
        for j, value in enumerate(row):
            found = jnp.where((z == i) & (core == j), jnp.int32(value), found)
    return found


def partial_body(*refs, plan, samples, peers):
    stat_refs, effect_ref, g_ref, out_refs = (
        refs[:peers], refs[peers], refs[peers + 1], refs[peers + 2 :],
    )
    stats = stat_refs[0][...]
    for ref in stat_refs[1:]:
        stats = stats + ref[...]
    mean, inverse_spread = moments(stats, samples)
    if len(out_refs) > len(plan):
        out_refs[-1][0:1, :] = mean
        out_refs[-1][1:2, :] = inverse_spread
    z, core = place()
    share = out_refs[0].shape[0]
    scaled, centers = [], []
    for table, mine in plan:
        block = block_of(table, z, core if mine else 1 - core)
        rows = effect_ref[pl.ds(pl.multiple_of(block * share, share), share), :]
        one = (rows.astype(F32) * inverse_spread).astype(BF16)
        scaled.append(one)
        centers.append(jnp.sum(one.astype(F32) * mean, axis=1, keepdims=True))
    left = jnp.concatenate(scaled, axis=0) if len(plan) > 1 else scaled[0]
    width = min(256, g_ref.shape[0])
    for at in range(0, g_ref.shape[0], width):
        product = lax.dot_general(
            left, g_ref[at : at + width, :], (((1,), (1,)), ((), ())), preferred_element_type=F32
        )
        for k, center in enumerate(centers):
            piece = product[k * share : (k + 1) * share] - center
            out_refs[k][:, at : at + width] = piece.astype(out_refs[k].dtype)


def chip_sum_body(keep_ref, arrived_ref, sum_ref, wire_ref):
    total = keep_ref[...] + arrived_ref[...].astype(F32)
    sum_ref[...] = total
    wire_ref[...] = total.astype(BF16)


def full_sum_body(keep_ref, arrived_ref, *refs):
    c_ref = refs[-1]
    c_ref[...] = (keep_ref[...] + arrived_ref[...].astype(F32)).astype(BF16)


def product(c, moment_ref, g_ref, out_refs):
    rows, cols = c.shape[0], g_ref.shape[1]
    wide = c.astype(F32)
    total = jnp.sum(wide, axis=1, keepdims=True)
    square = jnp.sum(wide * wide, axis=1, keepdims=True)
    width = min(512, cols)
    for at in range(0, cols, width):
        block = jnp.dot(c, g_ref[:, at : at + width], preferred_element_type=F32)
        block = block - total * moment_ref[0:1, at : at + width]
        for out_ref in out_refs:
            put(out_ref, at, block)
    diagonal = jnp.where(eye(rows), square, jnp.zeros((rows, LANES), F32))
    for out_ref in out_refs:
        put_tail(out_ref, jnp.sum(diagonal, axis=0, keepdims=True))


def eye(rows):
    row = lax.broadcasted_iota(jnp.int32, (rows, LANES), 0)
    return row == lax.broadcasted_iota(jnp.int32, (rows, LANES), 1)


def put(ref, at, block):
    rows = block.shape[0]
    for k in range(0, block.shape[1], LANES):
        start = (at + k) // LANES * rows
        ref[start : start + rows, :] = block[:, k : k + LANES].astype(ref.dtype)


def get(ref, at, rows):
    start = at // LANES * rows
    return ref[start : start + rows, :].astype(F32)


def put_tail(ref, square):
    high = square.astype(BF16).astype(F32)
    row = lax.broadcasted_iota(jnp.int32, (TAIL, LANES), 0)
    tail = jnp.where(row == 0, high, jnp.where(row == 1, square - high, jnp.zeros_like(square)))
    ref[ref.shape[0] - TAIL :, :] = tail.astype(ref.dtype)


def tail_sum(ref):
    tail = ref[ref.shape[0] - TAIL :, :].astype(F32)
    return tail[0:1, :] + tail[1:2, :]


def product_body(c_ref, moment_ref, g_ref, *out_refs):
    product(c_ref[...], moment_ref, g_ref, out_refs)


def pick_body(own_ref, other_ref, moment_ref, g_ref, out_ref, *, core_with_own):
    _, core = place()
    own, other = own_ref[...].astype(F32), other_ref[...].astype(F32)
    c = jnp.where(core == core_with_own, own, other).astype(BF16)
    product(c, moment_ref, g_ref, [out_ref])


def relay_body(held_ref, one_ref, out_ref):
    body = out_ref.shape[0] - TAIL
    out_ref[:body, :] = (held_ref[:body, :] + one_ref[:body, :].astype(F32)).astype(BF16)
    put_tail(out_ref, tail_sum(held_ref) + tail_sum(one_ref))


def finish_body(mine_ref, one_ref, two_ref, three_ref, four_ref, moment_ref, out_hbm, out_ref, sems, *, samples):
    z, core = place()
    rows, cols = out_ref.shape
    chunks = sems.shape[0]
    step = cols // chunks
    relayed = (core == 1) & ((z == 1) | (z == 2))

    def finish(refs):
        square = tail_sum(refs[0])
        for ref in refs[1:]:
            square = square + tail_sum(ref)
        square = jnp.sum(jnp.where(eye(rows), square, 0.0), axis=1, keepdims=True)
        scale = lax.rsqrt(square / samples + EPSILON) / math.sqrt(samples)
        for k in range(chunks):
            for at in range(k * step, (k + 1) * step, LANES):
                total = get(refs[0], at, rows)
                for ref in refs[1:]:
                    total = total + get(ref, at, rows)
                out_ref[:, at : at + LANES] = total * scale * moment_ref[1:2, at : at + LANES]
            copy(k).start()

    def copy(k):
        part = pl.ds(k * step, step)
        return pltpu.make_async_copy(out_ref.at[:, part], out_hbm.at[:, part], sems.at[k])

    @pl.when(jnp.logical_not(relayed))
    def _():
        finish([mine_ref, one_ref, two_ref, three_ref])

    @pl.when(relayed)
    def _():
        finish([mine_ref, three_ref, four_ref])

    for k in range(chunks):
        copy(k).wait()


def exchange(x, axis, k):
    return lax.ppermute(x, axis, [(i, i ^ k) for i in range(lax.axis_size(axis))])


def routed(x, *routes):
    peers = lax.axis_size("mrk")
    pairs = [
        (source * peers + m, target * peers + m)
        for m in range(peers)
        for source, target in routes[m % 2]
    ]
    return lax.ppermute(x, ("smp", "mrk"), pairs)


def small_mesh(genotypes, effect_class, effect_table):
    peers = lax.axis_size("smp")
    samples = genotypes.shape[0] * peers
    here, markers = genotypes.shape
    pheno = effect_table.shape[1]
    share = pheno // peers
    work = 2 * share * here * markers

    stats, held = marker_stats(genotypes)
    stats = [stats] + [exchange(stats, "smp", k) for k in (3, 2, 1)]
    effects = marker_effects(effect_class, effect_table)

    half = [shape((share, here), BF16)] * 2 + [shape((share, here), F32)] * 2
    plan = [(FIRST, False), (SECOND, False), (FIRST, True), (SECOND, True)]
    send_a, send_b, keep_a, keep_b, moment = call(
        functools.partial(partial_body, plan=plan, samples=samples, peers=peers),
        [*half, shape((2, markers), F32)], [*stats, effects, held],
        flops=4 * work, moved=2 * here * markers,
    )

    def chip_sum(keep, arrived):
        return call(chip_sum_body, [half[2], half[0]], [keep, arrived])

    def full_sum(keep, arrived, *earlier):
        return call(full_sum_body, half[0], [keep, arrived, *earlier])

    sum_a, wire_a = chip_sum(keep_a, exchange(send_a, "mrk", 1))
    far_a = exchange(wire_a, "mrk", 2)
    sum_b, wire_b = chip_sum(keep_b, exchange(send_b, "mrk", 1))
    far_b = exchange(wire_b, "mrk", 2)

    length = share * markers // LANES + TAIL
    piece, wide_piece = shape((length, LANES), BF16), shape((length, LANES), F32)

    def make(body, outs, inputs):
        return call(body, outs, [*inputs, moment, held], flops=work, moved=2 * here * markers)

    around = ((0, 1), (1, 3), (2, 0), (3, 2))
    outer, nearest = ((0, 3), (3, 0)), ((0, 1), (1, 0), (2, 3), (3, 2))
    inner = ((1, 2), (2, 1))
    own_a = full_sum(sum_a, far_a)
    (go1,) = make(product_body, [piece], [own_a])
    got1 = routed(go1, outer + inner, around)
    other_a = exchange(own_a, "mrk", 1)
    go2, held2 = make(product_body, [piece, wide_piece], [other_a])
    got2 = routed(go2, ((0, 2), (1, 3), (2, 0), (3, 1)), outer)
    own_b = full_sum(sum_b, far_b, go2)
    other_b = exchange(own_b, "mrk", 1)
    go3 = make(functools.partial(pick_body, core_with_own=0), piece, [own_b, other_b])
    got3 = routed(go3, nearest, nearest)
    go4 = call(relay_body, piece, [held2, got1])
    got4 = routed(go4, (), inner)
    mine = make(functools.partial(pick_body, core_with_own=1), wide_piece, [own_b, other_b])
    return call(
        functools.partial(finish_body, samples=samples),
        shape((share, markers), F32),
        [mine, got1, got2, got3, got4, moment], moved=8 * share * markers,
        scratch=[pltpu.VMEM((share, markers), F32), pltpu.SemaphoreType.DMA((4,))],
        out_spaces=pl.BlockSpec(memory_space=pl.ANY),
    )


def any_mesh(genotypes, effect_class, effect_table):
    samples = genotypes.shape[0] * lax.axis_size("smp")
    mean, inverse_spread = moments(lax.psum(marker_stats(genotypes)[0], "smp"), samples)
    effects = marker_effects(effect_class, effect_table)
    scaled = (effects.astype(F32) * inverse_spread).astype(BF16)
    center = jnp.sum(scaled.astype(F32) * mean, axis=1, keepdims=True)
    partial_sum = lax.dot_general(
        scaled, genotypes, (((1,), (1,)), ((), ())), preferred_element_type=F32
    )
    c = lax.psum(partial_sum - center, "mrk")
    spread = lax.psum(jnp.sum(jnp.square(c), axis=1, keepdims=True), "smp") / samples
    standard = (c * lax.rsqrt(spread + EPSILON)).astype(BF16)
    summed = lax.psum_scatter(
        jnp.dot(standard, genotypes, preferred_element_type=F32),
        "smp", scatter_dimension=0, tiled=True,
    )
    return summed * inverse_spread / math.sqrt(samples)


def solution(mesh):
    small = mesh.shape["smp"] == 4 and mesh.shape["mrk"] == 4
    return jax.shard_map(
        small_mesh if small else any_mesh,
        mesh=mesh,
        in_specs=(P("smp", ("grp", "mrk")), P(("grp", "mrk")), P("grp", None)),
        out_specs=P("smp", ("grp", "mrk")),
        check_vma=False,
    )
```
